128 devices in a mesh: rows: 16 (over z, x_hi, core), cols: 8 (over y, x_lo).
Axes of the slice: x: 4 (x_hi: 2, x_lo: 2; x = x_hi * 2 + x_lo), y: 4, z: 4, core: 2. Of those that a mesh axis runs over, the one named last changes fastest.
Arguments:
- gradient: float32 [12288, 28672], P('rows', 'cols'), may hold values from -6 to 6
- basis: float32 [16, 28672, 128], P('rows', 'cols'), may hold values from -0.03125 to 0.03125
- panel_index: int32 [4], replicated, may hold values from 0 to 15, as said below
- input_eigen: float32 [8192], replicated, may hold values from 0.1 to 3
- output_eigen: float32 [28672], replicated, may hold values from 0.1 to 3
- input_pick: int32 [4, 128], replicated, may hold values from 0 to 8191
- output_pick: int32 [4, 128], replicated, may hold values from 0 to 28671
Outputs:
- preconditioned: float32 [12288, 28672], P('rows', 'cols')
The draws below stay inside these ranges and needn't reach their ends.
Inputs may be any that keep to these rules, and one draw needn't show every extreme that they name: `panel_index`: the 4 entries are distinct.
All inputs are finite; a program needn't handle non-finite values.
Results may differ from the reference program's by a relative error of at most 0.0001.
Values sent between devices are 32-bit elements; how exact they have to be, the bound alone decides.
No kernel may reach another device: no remote copies, remote signals or barrier semaphores. Data moves between devices by JAX's collectives and lax.ppermute only.
A program may use at most 128 MiB of HBM per device.

```python
import math
import jax
import jax.numpy as jnp
from jax import lax

D = 8192
M = 28672
PANEL = 128
NSEL = 4
PSTOCK = 16
R = 12288


def draw_panel_index(key, part):
    middle = jax.random.permutation(jax.random.fold_in(key, 11), PSTOCK - 2)[:NSEL - 2] + 1
    ends = jnp.array([0, PSTOCK - 1], jnp.int32)
    picked = jnp.concatenate([ends, middle.astype(jnp.int32)])
    order = jax.random.permutation(jax.random.fold_in(key, 13), NSEL)
    return picked[order].astype(jnp.int32)


def place_ends(values, own_key, smallest, high):
    dims = values.shape
    place = [jax.random.randint(jax.random.fold_in(own_key, axis), (), 0, dims[axis]) for axis in range(len(dims))]
    values = values.at[tuple(place)].set(smallest)
    longest = dims.index(max(dims))
    place[longest] = (place[longest] + 1) % dims[longest]
    return values.at[tuple(place)].set(high)


def block_scale(own_key, extent, split, least, high):
    gain, own = 1.0, jax.random.fold_in(own_key, 6)
    for position, shards_of in split:
        heights = jnp.exp(jax.random.uniform(jax.random.fold_in(own, position), (shards_of,), jnp.float32, least / len(split), high / len(split)))
        gain = gain * jnp.repeat(heights, extent[position] // shards_of).reshape([-1 if axis == position else 1 for axis in range(len(extent))])
    return gain


def noise(own_key, dims, deviation, most, split=(), held_as=jnp.bfloat16):
    level = block_scale(own_key, dims, split, -0.22, 0.18) if split else 1.0
    values = jax.random.normal(own_key, dims, jnp.float32) * deviation * level
    return jnp.minimum(jnp.maximum(values, -most), most).astype(held_as)


def setup_inputs(seed: int = 0) -> dict:
    seeds = jax.random.split(jax.random.key(seed), 8)
    return {
        "gradient": noise(seeds[0], (R, M), 1.0, 6.0, ((0, 16), (1, 8)), jnp.float32),
        "basis": noise(seeds[1], (PSTOCK, M, PANEL), M ** -0.5, 0.03125, ((0, 16), (1, 8)), jnp.float32),
        "panel_index": draw_panel_index(jax.random.fold_in(seeds[7], 71), 0),
        "input_eigen": jnp.clip(jnp.exp(jax.random.uniform(seeds[3], (D,), jnp.float32, math.log(0.1), math.log(3.0))), 0.1, 3.0),
        "output_eigen": jnp.clip(jnp.exp(jax.random.uniform(seeds[4], (M,), jnp.float32, math.log(0.1), math.log(3.0))), 0.1, 3.0),
        "input_pick": place_ends(jax.random.randint(seeds[5], (NSEL, PANEL), 0, D), jax.random.fold_in(seeds[5], 1), 0, D - 1).astype(jnp.int32),
        "output_pick": place_ends(jax.random.randint(seeds[6], (NSEL, PANEL), 0, M), jax.random.fold_in(seeds[6], 1), 0, M - 1).astype(jnp.int32),
    }


def reference(gradient, basis, panel_index, input_eigen, output_eigen, input_pick, output_pick):
    result = jnp.zeros(gradient.shape, jnp.float32)
    for number in range(NSEL):
        chosen = basis[panel_index[number]]
        projected = jnp.dot(gradient, chosen, precision=lax.Precision.HIGHEST, preferred_element_type=jnp.float32)
        damped = input_eigen[input_pick[number]] * output_eigen[output_pick[number]] + 0.05
        scaled = projected / damped[None, :]
        result = result + jnp.dot(scaled, chosen.T, precision=lax.Precision.HIGHEST, preferred_element_type=jnp.float32)
    return result
```

```python
import jax
import jax.numpy as jnp
from jax import lax
from jax.sharding import PartitionSpec as P

NSEL = 4
PANEL = 128
PLANES = 4
COLS = 8
HIGH = lax.Precision.HIGH


CORE = [(r, r ^ 1) for r in range(16)]
XPAIR = [(r, r ^ 2) for r in range(16)]
RING = [(r, ((r // 4 + (1 if r % 2 == 0 else 3)) % 4) * 4 + r % 4) for r in range(16)]


def ordered(first, mine, other):
    low = jnp.where(first, mine, other)
    high = jnp.where(first, other, mine)
    return jnp.concatenate([low, high], axis=0)


def scatter_panels(basis, panel_index):
    depth = basis.shape[1] // 16
    pieces = lax.all_to_all(basis.reshape(16, depth, PANEL), "rows", 0, 0)
    return [lax.dynamic_index_in_dim(pieces, panel_index[k], 0, keepdims=False) for k in range(NSEL)]


def dot(a, b):
    return jnp.dot(a, b, precision=HIGH, preferred_element_type=jnp.float32)


def shards(gradient, basis, panel_index, input_eigen, output_eigen, input_pick, output_pick):
    rows, width = gradient.shape
    quarter = width // PLANES
    me = lax.axis_index("rows")
    z, x, core = me // 4, (me // 2) % 2, me % 2
    even = core == 0

    damped = (input_eigen[input_pick] * output_eigen[output_pick] + 0.05).reshape(-1)
    damped = jnp.where(even, damped, jnp.roll(damped, 2 * PANEL))

    chosen = scatter_panels(basis, panel_index)
    low = jnp.concatenate(chosen[:2], axis=1)
    high = jnp.concatenate(chosen[2:], axis=1)
    mine = jnp.where(even, low, high)
    give = jnp.where(even, high, low)
    half = ordered(even, mine, lax.ppermute(give, "rows", CORE))
    held = ordered(x == 0, half, lax.ppermute(half, "rows", XPAIR))

    own, oth = [held], []
    for step in range(PLANES):
        oth.append(lax.ppermute(own[step], "rows", CORE))
        if step < PLANES - 1:
            own.append(lax.ppermute(own[step], "rows", RING))

    way = jnp.where(even, 1, -1)
    p_own = p_oth = None
    v_own = jnp.zeros((width, 2 * PANEL), jnp.float32)
    v_oth = jnp.zeros((width, 2 * PANEL), jnp.float32)
    for step in range(PLANES):
        at_own = ((z - step * way + 4) % 4) * quarter
        at_oth = ((z + step * way + 4) % 4) * quarter
        a = dot(lax.dynamic_slice(gradient, (0, at_own), (rows, quarter)), own[step])
        b = dot(lax.dynamic_slice(gradient, (0, at_oth), (rows, quarter)), oth[step])
        p_own = a if step == 0 else p_own + a
        p_oth = b if step == 0 else p_oth + b
        v_own = lax.dynamic_update_slice(v_own, own[step], (at_own, 0))
        v_oth = lax.dynamic_update_slice(v_oth, oth[step], (at_oth, 0))

    partial = jnp.concatenate([p_own, p_oth], axis=1)
    blocks = lax.all_to_all(partial.reshape(COLS, rows // COLS, NSEL * PANEL), "cols", 0, 0)
    scaled = jnp.sum(blocks, axis=0) / damped[None, :]
    scaled = jnp.broadcast_to(scaled[None], (COLS,) + scaled.shape)
    scaled = lax.all_to_all(scaled, "cols", 0, 0).reshape(rows, NSEL * PANEL)
    v = jnp.concatenate([v_own, v_oth], axis=1)
    return lax.dot_general(
        scaled, v, (((1,), (1,)), ((), ())), precision=HIGH, preferred_element_type=jnp.float32
    )


def solution(mesh):
    in_specs = (P("rows", "cols"), P("rows", "cols", None), P(), P(), P(), P(), P())
    out_specs = P("rows", "cols")
    return jax.shard_map(shards, mesh=mesh, in_specs=in_specs, out_specs=out_specs, check_vma=False)
```

```python
import functools

import jax
import jax.numpy as jnp
from jax import lax
from jax.experimental import pallas as pl
from jax.experimental.pallas import tpu as pltpu
from jax.sharding import PartitionSpec as P


NSEL = 4
PANEL = 128
PAIR = 2 * PANEL
PLANES = 4
COLS = 8
HALVES = 2
TILE = 384
DEPTH = 4
CHUNKS = ((0, 512), (512, 384))
BF = jnp.bfloat16
F32 = jnp.float32


CORE = [(r, r ^ 1) for r in range(16)]
XPAIR = [(r, r ^ 2) for r in range(16)]
RING = [(r, ((r // 4 + (1 if r % 2 == 0 else 3)) % 4) * 4 + r % 4) for r in range(16)]

VM = pl.BlockSpec()
SM = pl.BlockSpec(memory_space=pltpu.SMEM)
HBM = pl.BlockSpec(memory_space=pltpu.HBM)


def stay(value):
    return pltpu.with_memory_space_constraint(value, pltpu.HBM)


def ordered(first, mine, other):
    low = jnp.where(first, mine, other)
    high = jnp.where(first, other, mine)
    return jnp.concatenate([low, high], axis=0)


def two_terms(value):
    high = value.astype(BF)
    return high, (value - high.astype(F32)).astype(BF)


def split_body(g_ref, out_ref):
    quarter = g_ref.shape[1] // PLANES
    for z in range(PLANES):
        high, low = two_terms(g_ref[:, z * quarter : (z + 1) * quarter])
        out_ref[z, 0] = high
        out_ref[z, 1] = low


def split_gradient(gradient, tile=96):
    rows, width = gradient.shape
    quarter = width // PLANES
    return pl.pallas_call(
        split_body,
        grid=(rows // tile,),
        out_shape=pltpu.HBM((PLANES, 2, rows, quarter), BF),
        in_specs=[pl.BlockSpec((tile, width), lambda i: (i, 0))],
        out_specs=pl.BlockSpec((PLANES, 2, tile, quarter), lambda i: (0, 0, i, 0)),
        compiler_params=pltpu.CompilerParams(vmem_limit_bytes=16 << 20),
        cost_estimate=pl.CostEstimate(flops=rows * width * 4, bytes_accessed=rows * width * 8, transcendentals=0),
        name="split",
    )(stay(gradient))


def pick_body(at_ref, pieces_ref, a_ref, b_ref, give_ref):
    core = at_ref[NSEL]
    a_ref[...] = pieces_ref[at_ref[2 * core]]
    b_ref[...] = pieces_ref[at_ref[2 * core + 1]]
    give_ref[0] = pieces_ref[at_ref[2 - 2 * core]]
    give_ref[1] = pieces_ref[at_ref[3 - 2 * core]]


def pick(at, pieces):
    one = jax.ShapeDtypeStruct(pieces.shape[1:], F32)
    two = jax.ShapeDtypeStruct((2, *pieces.shape[1:]), F32)
    return pl.pallas_call(
        pick_body,
        out_shape=[one, one, two],
        in_specs=[SM, VM],
        out_specs=[VM] * 3,
        compiler_params=pltpu.CompilerParams(vmem_limit_bytes=8 << 20),
        cost_estimate=pl.CostEstimate(flops=1, bytes_accessed=pieces.size, transcendentals=0),
        name="pick",
    )(at, pieces)


def project_body(first, step, at_ref, g_ref, own_a, own_b, oth_a, oth_b, *rest):
    p_in = None if first else rest[0]
    p_ref, v_all, terms, stage, sems, keep = rest[-6:]
    rows, quarter = g_ref.shape[2:]

    def copies(side, row):
        q, take = at_ref[side * PLANES + step], pl.ds(row, TILE)
        return [
            pltpu.make_async_copy(g_ref.at[q, t, take], stage.at[side, t, take], sems.at[side, t, row // TILE])
            for t in range(2)
        ]

    tiles = [(side, row) for side in range(2) for row in range(0, rows, TILE)]
    for tile in tiles:
        for move in copies(*tile):
            move.start()
    saves = []
    for side, pair in enumerate(((own_a, own_b), (oth_a, oth_b))):
        for i, v_ref in enumerate(pair):
            lanes = slice(i * PANEL, (i + 1) * PANEL)
            terms[side, 0, :, lanes], terms[side, 1, :, lanes] = two_terms(v_ref[...])
        save = pltpu.make_async_copy(
            terms.at[side], v_all.at[side, :, pl.ds(step * quarter, quarter)], keep.at[side])
        save.start()
        saves.append(save)
    for side, row in tiles:
        lanes = slice(side * PAIR, (side + 1) * PAIR)
        take = slice(row, row + TILE)
        for move in copies(side, row):
            move.wait()
        both = stage[side, :, take].reshape(2 * TILE, quarter)
        wide = jnp.dot(both, terms[side, 0], preferred_element_type=F32)
        total = jnp.dot(both[:TILE], terms[side, 1], preferred_element_type=F32) + wide[TILE:]
        total += wide[:TILE]
        if not first:
            total += p_in[take, lanes]
        p_ref[take, lanes] = total
    for save in saves:
        save.wait()


def project(step, at, g, own, oth, state):
    rows, quarter = g.shape[2:]
    ins = [at, stay(g), *own, *oth, *state[:1], *[stay(v) for v in state[1:]]]
    return pl.pallas_call(
        functools.partial(project_body, not state, step),
        out_shape=[
            jax.ShapeDtypeStruct((rows, 2 * PAIR), F32),
            pltpu.HBM((2, 2, PLANES * quarter, PAIR), BF),
        ],
        in_specs=[SM, HBM] + [VM] * 4 + ([VM, HBM] if state else []),
        out_specs=[VM, HBM],
        scratch_shapes=[
            pltpu.VMEM((2, 2, quarter, PAIR), BF),
            pltpu.VMEM((2, 2, rows, quarter), BF),
            pltpu.SemaphoreType.DMA((2, 2, rows // TILE)),
            pltpu.SemaphoreType.DMA((2,)),
        ],
        input_output_aliases={6: 0, 7: 1} if state else {},
        compiler_params=pltpu.CompilerParams(vmem_limit_bytes=24 << 20),
        cost_estimate=pl.CostEstimate(
            flops=rows * quarter * PAIR * 12, bytes_accessed=rows * quarter * 8, transcendentals=0),
        name="project",
    )(*ins)


def expand_body(row0, at_ref, s_ref, v_all, *rest):
    out_ref, terms, stage, in_sems, sems = rest[-5:]
    quarter = v_all.shape[2] // PLANES
    rows = s_ref.shape[0]
    blocks = [(s, c) for s in range(PLANES) for c in range(len(CHUNKS))]

    def fetch(k):
        s, c = blocks[k]
        at, long = CHUNKS[c]
        moves = []
        for side, step in enumerate((s, (PLANES - s) % PLANES)):
            for t in range(2):
                moves.append(pltpu.make_async_copy(
                    v_all.at[side, t, pl.ds(step * quarter + at, long)],
                    terms.at[k % DEPTH, side, t, pl.ds(0, long)],
                    in_sems.at[k % DEPTH, side, t]))
        return moves

    def put(k):
        s, c = blocks[k]
        at, long = CHUNKS[c]
        cols = pl.ds(pl.multiple_of(at_ref[s] * quarter + at, 128), long)
        return pltpu.make_async_copy(
            stage.at[k % 2, :, :, pl.ds(0, long)], out_ref.at[:, pl.ds(row0, stage.shape[2]), cols], sems.at[k % 2])

    nt = lambda a, b: lax.dot_general(a, b, (((1,), (1,)), ((), ())), preferred_element_type=F32)
    for k in range(DEPTH):
        for move in fetch(k):
            move.start()
    both = jnp.concatenate(two_terms(s_ref[...]), axis=0)
    for k, (s, c) in enumerate(blocks):
        long = CHUNKS[c][1]
        for move in fetch(k):
            move.wait()
        vh, vl = (
            jnp.concatenate([terms[k % DEPTH, side, t, 0:long] for side in range(2)], axis=1) for t in range(2))
        wide = nt(both, vh)
        total = nt(both[:rows], vl) + wide[rows:]
        total += wide[:rows]
        if k >= 2:
            put(k - 2).wait()
        stage[k % 2, :, :, 0:long] = total.reshape(stage.shape[1], stage.shape[2], long)
        put(k).start()
        if k + DEPTH < len(blocks):
            for move in fetch(k + DEPTH):
                move.start()
    put(len(blocks) - 2).wait()
    put(len(blocks) - 1).wait()


def expand(at, scaled, v, out, row0, shape):
    count = scaled.shape[0]
    ins = [at, scaled, stay(v)] + ([] if out is None else [out])
    return pl.pallas_call(
        functools.partial(expand_body, row0),
        out_shape=jax.ShapeDtypeStruct(shape, F32),
        in_specs=[SM, VM, HBM] + ([] if out is None else [HBM]),
        out_specs=HBM,
        scratch_shapes=[
            pltpu.VMEM((DEPTH, 2, 2, 512, PAIR), BF),
            pltpu.VMEM((2, shape[0], count // shape[0], 512), F32),
            pltpu.SemaphoreType.DMA((DEPTH, 2, 2)),
            pltpu.SemaphoreType.DMA((2,)),
        ],
        input_output_aliases={} if out is None else {3: 0},
        compiler_params=pltpu.CompilerParams(vmem_limit_bytes=24 << 20),
        cost_estimate=pl.CostEstimate(
            flops=count * shape[2] * 512 * 6, bytes_accessed=count * shape[2] * 4, transcendentals=0),
        name="expand",
    )(*ins)


def shards(gradient, basis, panel_index, input_eigen, output_eigen, input_pick, output_pick):
    rows, width = gradient.shape
    me = lax.axis_index("rows")
    z, x, core = me // 4, (me // 2) % 2, me % 2
    even = core == 0
    way = jnp.where(even, 1, -1)

    damped = (input_eigen[input_pick] * output_eigen[output_pick] + 0.05).reshape(-1)
    damped = jnp.where(even, damped, jnp.roll(damped, PAIR))

    pieces = lax.all_to_all(basis.reshape(16, -1, PANEL), "rows", 0, 0)
    g = split_gradient(gradient)
    pieces, g = lax.optimization_barrier((pieces, g))
    mine_a, mine_b, give = pick(jnp.append(panel_index, core).astype(jnp.int32), pieces)
    got = lax.ppermute(give, "rows", CORE)
    halves = [ordered(even, mine_a, got[0]), ordered(even, mine_b, got[1])]
    own = [[], []]
    for c, half in enumerate(halves):
        own[c].append(ordered(x == 0, half, lax.ppermute(half, "rows", XPAIR)))

    at = jnp.arange(PLANES, dtype=jnp.int32) * way.astype(jnp.int32)
    at = jnp.concatenate([(z - at + 4) % 4, (z + at + 4) % 4])
    state, waiting = (), None
    for step in range(PLANES):
        oth = [None, None]
        for c in range(2):
            held = own[c][step]
            if c == 0 and waiting is not None:
                _, last_oth = waiting[1:]
                if state:
                    held, last_oth[0], p = lax.optimization_barrier((held, last_oth[0], state[0]))
                    state = (p, *state[1:])
                else:
                    held, last_oth[0] = lax.optimization_barrier((held, last_oth[0]))
            if step < PLANES - 1:
                own[c].append(lax.ppermute(held, "rows", RING))
            oth[c] = lax.ppermute(held, "rows", CORE)
        if waiting is not None:
            state = project(waiting[0], at, g, waiting[1], waiting[2], state)
        waiting = (step, [own[0][step], own[1][step]], oth)
    p, v = project(waiting[0], at, g, waiting[1], waiting[2], state)

    blocks = lax.all_to_all(p.reshape(COLS, rows // COLS, NSEL * PANEL), "cols", 0, 0)
    scaled = jnp.sum(blocks, axis=0) / damped[None, :]
    part = rows // HALVES
    own_rows = rows // COLS // HALVES
    out = None
    gathered = []
    for h in range(HALVES):
        piece = scaled[h * own_rows : (h + 1) * own_rows]
        piece = jnp.broadcast_to(piece[None], (COLS,) + piece.shape)
        gathered.append(lax.all_to_all(piece, "cols", 0, 0).reshape(part, NSEL * PANEL))
    for h in range(HALVES):
        out = expand(at, gathered[h], v, out, h * own_rows, (COLS, rows // COLS, width))
    return out.reshape(rows, width)


def solution(mesh):
    in_specs = (P("rows", "cols"), P("rows", "cols", None), P(), P(), P(), P(), P())
    out_specs = P("rows", "cols")

    return jax.shard_map(shards, mesh=mesh, in_specs=in_specs, out_specs=out_specs, check_vma=False)
```

```python
import jax
import jax.numpy as jnp
from jax import lax
from jax.experimental import pallas as pl
from jax.experimental.pallas import tpu as pltpu
from jax.sharding import PartitionSpec as P


NSEL = 4
PANEL = 128
PAIR = 2 * PANEL
PLANES = 4
COLS = 8
F32 = jnp.float32


CORE = [(r, r ^ 1) for r in range(16)]
XPAIR = [(r, r ^ 2) for r in range(16)]
RING = [(r, ((r // 4 + (1 if r % 2 == 0 else 3)) % 4) * 4 + r % 4) for r in range(16)]

VM = pl.BlockSpec()
SM = pl.BlockSpec(memory_space=pltpu.SMEM)
HBM = pl.BlockSpec(memory_space=pltpu.HBM)


def stay(value):
    return pltpu.with_memory_space_constraint(value, pltpu.HBM)


def ordered(first, mine, other):
    low = jnp.where(first, mine, other)
    high = jnp.where(first, other, mine)
    return jnp.concatenate([low, high], axis=0)


def rotate_body(at_ref, *refs):
    for i in range(PLANES):
        refs[PLANES + i][...] = refs[i][...]


def rotate(at, gradient, tile=96):
    rows, width = gradient.shape
    quarter = width // PLANES
    spec = lambda i: pl.BlockSpec((tile, quarter), lambda r, at_ref: (r, at_ref[i]))
    return pl.pallas_call(
        rotate_body,
        grid_spec=pltpu.PrefetchScalarGridSpec(
            num_scalar_prefetch=1,
            grid=(rows // tile,),
            in_specs=[spec(i) for i in range(PLANES)],
            out_specs=[pl.BlockSpec((tile, quarter), lambda r, at_ref: (r, 0))] * PLANES,
        ),
        out_shape=[jax.ShapeDtypeStruct((rows, quarter), F32)] * PLANES,
        compiler_params=pltpu.CompilerParams(vmem_limit_bytes=16 << 20),
        cost_estimate=pl.CostEstimate(flops=1, bytes_accessed=rows * width * 8, transcendentals=0),
        name="rotate",
    )(at, *[stay(gradient)] * PLANES)


def pick_body(at_ref, pieces_ref, a_ref, b_ref, give_ref):
    core = at_ref[NSEL]
    a_ref[...] = pieces_ref[at_ref[2 * core]]
    b_ref[...] = pieces_ref[at_ref[2 * core + 1]]
    give_ref[0] = pieces_ref[at_ref[2 - 2 * core]]
    give_ref[1] = pieces_ref[at_ref[3 - 2 * core]]


def pick(at, pieces):
    one = jax.ShapeDtypeStruct(pieces.shape[1:], F32)
    two = jax.ShapeDtypeStruct((2, *pieces.shape[1:]), F32)
    return pl.pallas_call(
        pick_body,
        out_shape=[one, one, two],
        in_specs=[SM, VM],
        out_specs=[VM] * 3,
        compiler_params=pltpu.CompilerParams(vmem_limit_bytes=8 << 20),
        cost_estimate=pl.CostEstimate(flops=1, bytes_accessed=pieces.size, transcendentals=0),
        name="pick",
    )(at, pieces)


def place_body(at_ref, *refs):
    v_ref, sems = refs[-2:]
    quarter = refs[0].shape[0]
    moves = []
    for side in range(2):
        for step in range(PLANES):
            rows = pl.ds(pl.multiple_of(at_ref[side * PLANES + step] * quarter, 128), quarter)
            lanes = pl.ds(side * PAIR, PAIR)
            moves.append(pltpu.make_async_copy(refs[side * PLANES + step], v_ref.at[rows, lanes], sems.at[side, step]))
    for move in moves:
        move.start()
    for move in moves:
        move.wait()


def place(at, own, oth):
    quarter = own[0].shape[0]
    return pl.pallas_call(
        place_body,
        out_shape=pltpu.HBM((PLANES * quarter, 2 * PAIR), F32),
        in_specs=[SM] + [VM] * (2 * PLANES),
        out_specs=HBM,
        scratch_shapes=[pltpu.SemaphoreType.DMA((2, PLANES))],
        compiler_params=pltpu.CompilerParams(vmem_limit_bytes=8 << 20),
        cost_estimate=pl.CostEstimate(flops=1, bytes_accessed=quarter * PAIR * 64, transcendentals=0),
        name="place",
    )(at, *own, *oth)


def dot(a, b):
    return jnp.dot(a, b, precision=lax.Precision.HIGH, preferred_element_type=F32)


def shards(gradient, basis, panel_index, input_eigen, output_eigen, input_pick, output_pick):
    rows, _ = gradient.shape
    me = lax.axis_index("rows")
    z, x, core = me // 4, (me // 2) % 2, me % 2
    even = core == 0
    way = jnp.where(even, 1, -1)

    damped = (input_eigen[input_pick] * output_eigen[output_pick] + 0.05).reshape(-1)
    damped = jnp.where(even, damped, jnp.roll(damped, PAIR))

    pieces = lax.all_to_all(basis.reshape(16, -1, PANEL), "rows", 0, 0)
    at = jnp.arange(PLANES, dtype=jnp.int32) * way.astype(jnp.int32)
    at = jnp.concatenate([(z - at + 4) % 4, (z + at + 4) % 4])
    pieces, *g = lax.optimization_barrier((pieces, *rotate(at, gradient)))
    mine_a, mine_b, give = pick(jnp.append(panel_index, core).astype(jnp.int32), pieces)
    got = lax.ppermute(give, "rows", CORE)
    halves = [ordered(even, mine_a, got[0]), ordered(even, mine_b, got[1])]
    own = [[], []]
    for c, half in enumerate(halves):
        own[c].append(ordered(x == 0, half, lax.ppermute(half, "rows", XPAIR)))

    v_own, v_oth, total, waiting = [], [], None, None

    def product(step, own, oth, total):
        mine, other = jnp.concatenate(own, axis=1), jnp.concatenate(oth, axis=1)
        v_own.append(mine)
        v_oth.append(other)
        mine, other = dot(g[step], mine), dot(g[-step % PLANES], other)
        return (mine, other) if total is None else (total[0] + mine, total[1] + other)

    for step in range(PLANES):
        oth = [None, None]
        for c in range(2):
            held = own[c][step]
            if c == 0 and waiting is not None:
                last_oth = waiting[2]
                if total is not None:
                    held, last_oth[0], *total = lax.optimization_barrier((held, last_oth[0], *total))
                else:
                    held, last_oth[0] = lax.optimization_barrier((held, last_oth[0]))
            if step < PLANES - 1:
                own[c].append(lax.ppermute(held, "rows", RING))
            oth[c] = lax.ppermute(held, "rows", CORE)
        if waiting is not None:
            total = product(*waiting, total)
        waiting = (step, [own[0][step], own[1][step]], oth)
    total = product(*waiting, total)
    p = jnp.concatenate(total, axis=1)
    v = place(at, v_own, v_oth)

    blocks = lax.all_to_all(p.reshape(COLS, rows // COLS, NSEL * PANEL), "cols", 0, 0)
    scaled = jnp.sum(blocks, axis=0) / damped[None, :]
    scaled = jnp.broadcast_to(scaled[None], (COLS,) + scaled.shape)
    scaled = lax.all_to_all(scaled, "cols", 0, 0).reshape(rows, NSEL * PANEL)
    return lax.dot_general(
        scaled, v, (((1,), (1,)), ((), ())), precision=lax.Precision.HIGH, preferred_element_type=F32
    )


def solution(mesh):
    in_specs = (P("rows", "cols"), P("rows", "cols", None), P(), P(), P(), P(), P())
    out_specs = P("rows", "cols")

    return jax.shard_map(shards, mesh=mesh, in_specs=in_specs, out_specs=out_specs, check_vma=False)
```

```python
import jax
import jax.numpy as jnp
from jax import lax
from jax.experimental import pallas as pl
from jax.experimental.pallas import tpu as pltpu
from jax.sharding import PartitionSpec as P


NSEL = 4
PANEL = 128
PAIR = 2 * PANEL
PLANES = 4
COLS = 8
F32 = jnp.float32


CORE = [(r, r ^ 1) for r in range(16)]
CHIPS = [[r for r in range(16) if r % 2 == core] for core in range(2)]
XPAIR = [(r, r ^ 2) for r in range(16)]
RING = [(r, ((r // 4 + (1 if r % 2 == 0 else 3)) % 4) * 4 + r % 4) for r in range(16)]

VM = pl.BlockSpec()
SM = pl.BlockSpec(memory_space=pltpu.SMEM)
HBM = pl.BlockSpec(memory_space=pltpu.HBM)


def stay(value):
    return pltpu.with_memory_space_constraint(value, pltpu.HBM)


def ordered(first, mine, other):
    low = jnp.where(first, mine, other)
    high = jnp.where(first, other, mine)
    return jnp.concatenate([low, high], axis=0)


def rotate_body(at_ref, *refs):
    for i in range(PLANES):
        refs[PLANES + i][...] = refs[i][...]


def rotate(at, gradient, tile=96):
    rows, width = gradient.shape
    quarter = width // PLANES
    spec = lambda i: pl.BlockSpec((tile, quarter), lambda r, at_ref: (r, at_ref[i]))
    return pl.pallas_call(
        rotate_body,
        grid_spec=pltpu.PrefetchScalarGridSpec(
            num_scalar_prefetch=1,
            grid=(rows // tile,),
            in_specs=[spec(i) for i in range(PLANES)],
            out_specs=[pl.BlockSpec((tile, quarter), lambda r, at_ref: (r, 0))] * PLANES,
        ),
        out_shape=[jax.ShapeDtypeStruct((rows, quarter), F32)] * PLANES,
        compiler_params=pltpu.CompilerParams(vmem_limit_bytes=16 << 20),
        cost_estimate=pl.CostEstimate(flops=1, bytes_accessed=rows * width * 8, transcendentals=0),
        name="rotate",
    )(at, *[stay(gradient)] * PLANES)


def pick_body(at_ref, pieces_ref, mine_ref, give_ref):
    core = at_ref[NSEL]
    for i in range(2):
        mine_ref[i] = pieces_ref[at_ref[2 * core + i] // 2]
        give_ref[i] = pieces_ref[at_ref[2 - 2 * core + i] // 2]


def pick(at, pieces):
    two = jax.ShapeDtypeStruct((2, *pieces.shape[1:]), F32)
    return pl.pallas_call(
        pick_body,
        out_shape=[two, two],
        in_specs=[SM, VM],
        out_specs=[VM] * 2,
        compiler_params=pltpu.CompilerParams(vmem_limit_bytes=8 << 20),
        cost_estimate=pl.CostEstimate(flops=1, bytes_accessed=pieces.size, transcendentals=0),
        name="pick",
    )(at, pieces)


def settle_body(at_ref, mine_ref, got_ref, *outs):
    core = at_ref[NSEL]
    for i, out in enumerate(outs):
        here = at_ref[2 * core + i] % 2 == core

        @pl.when(here)
        def _():
            out[...] = mine_ref[i]

        @pl.when(jnp.logical_not(here))
        def _():
            out[...] = got_ref[i]


def settle(at, mine, got):
    one = jax.ShapeDtypeStruct(mine.shape[1:], F32)
    return pl.pallas_call(
        settle_body,
        out_shape=[one, one],
        in_specs=[SM, VM, VM],
        out_specs=[VM] * 2,
        compiler_params=pltpu.CompilerParams(vmem_limit_bytes=8 << 20),
        cost_estimate=pl.CostEstimate(flops=1, bytes_accessed=mine.size * 8, transcendentals=0),
        name="settle",
    )(at, mine, got)


def place_body(at_ref, *refs):
    v_ref, sems = refs[-2:]
    quarter = refs[0].shape[0]
    moves = []
    for side in range(2):
        for step in range(PLANES):
            rows = pl.ds(pl.multiple_of(at_ref[side * PLANES + step] * quarter, 128), quarter)
            lanes = pl.ds(side * PAIR, PAIR)
            moves.append(pltpu.make_async_copy(refs[side * PLANES + step], v_ref.at[rows, lanes], sems.at[side, step]))
    for move in moves:
        move.start()
    for move in moves:
        move.wait()


def place(at, own, oth):
    quarter = own[0].shape[0]
    return pl.pallas_call(
        place_body,
        out_shape=pltpu.VMEM((PLANES * quarter, 2 * PAIR), F32),
        in_specs=[SM] + [VM] * (2 * PLANES),
        out_specs=VM,
        scratch_shapes=[pltpu.SemaphoreType.DMA((2, PLANES))],
        compiler_params=pltpu.CompilerParams(vmem_limit_bytes=8 << 20),
        cost_estimate=pl.CostEstimate(flops=1, bytes_accessed=quarter * PAIR * 64, transcendentals=0),
        name="place",
    )(at, *own, *oth)


def dot(a, b):
    return jnp.dot(a, b, precision=lax.Precision.HIGH, preferred_element_type=F32)


def shards(gradient, basis, panel_index, input_eigen, output_eigen, input_pick, output_pick):
    rows, _ = gradient.shape
    me = lax.axis_index("rows")
    z, x, core = me // 4, (me // 2) % 2, me % 2
    even = core == 0
    way = jnp.where(even, 1, -1)

    damped = (input_eigen[input_pick] * output_eigen[output_pick] + 0.05).reshape(-1)
    damped = jnp.where(even, damped, jnp.roll(damped, PAIR))

    pieces = lax.all_to_all(basis.reshape(8, -1, PANEL), "rows", 0, 0, axis_index_groups=CHIPS)
    at = jnp.arange(PLANES, dtype=jnp.int32) * way.astype(jnp.int32)
    at = jnp.concatenate([(z - at + 4) % 4, (z + at + 4) % 4])
    pieces, *g = lax.optimization_barrier((pieces, *rotate(at, gradient)))
    chosen = jnp.append(panel_index, core).astype(jnp.int32)
    mine, give = pick(chosen, pieces)
    half_a, half_b = settle(chosen, mine, lax.ppermute(give, "rows", CORE))

    def other_x(half):
        return ordered(x == 0, half, lax.ppermute(half, "rows", XPAIR))

    own, halves = [[other_x(half_a)], []], [half_b]
    for step in range(PLANES - 1):
        halves.append(lax.ppermute(halves[step], "rows", RING))
    own[1] = [other_x(half) for half in halves]

    v_own, v_oth, total, waiting = [], [], None, None

    def product(step, own, oth, total):
        mine, other = jnp.concatenate(own, axis=1), jnp.concatenate(oth, axis=1)
        v_own.append(mine)
        v_oth.append(other)
        mine, other = dot(g[step], mine), dot(g[-step % PLANES], other)
        return (mine, other) if total is None else (total[0] + mine, total[1] + other)

    for step in range(PLANES):
        oth = [None, None]
        for c in range(2):
            held = own[c][step]
            if c == 0 and waiting is not None:
                last_oth = waiting[2]
                if total is not None:
                    held, last_oth[0], *total = lax.optimization_barrier((held, last_oth[0], *total))
                else:
                    held, last_oth[0] = lax.optimization_barrier((held, last_oth[0]))
            if c == 0 and step < PLANES - 1:
                own[c].append(lax.ppermute(held, "rows", RING))
            oth[c] = lax.ppermute(held, "rows", CORE)
        if waiting is not None:
            total = product(*waiting, total)
        waiting = (step, [own[0][step], own[1][step]], oth)
    total = product(*waiting, total)
    p = jnp.concatenate(total, axis=1)
    v = place(at, v_own, v_oth)

    blocks = lax.all_to_all(p.reshape(COLS, rows // COLS, NSEL * PANEL), "cols", 0, 0)
    scaled = jnp.sum(blocks, axis=0) / damped[None, :]
    scaled = jnp.broadcast_to(scaled[None], (COLS,) + scaled.shape)
    scaled = lax.all_to_all(scaled, "cols", 0, 0).reshape(rows, NSEL * PANEL)
    return lax.dot_general(
        scaled, v, (((1,), (1,)), ((), ())), precision=lax.Precision.HIGH, preferred_element_type=F32
    )


def solution(mesh):
    in_specs = (P("rows", "cols"), P("rows", "cols", None), P(), P(), P(), P(), P())
    out_specs = P("rows", "cols")

    return jax.shard_map(shards, mesh=mesh, in_specs=in_specs, out_specs=out_specs, check_vma=False)
```

```python
import jax
import jax.numpy as jnp
from jax import lax
from jax.experimental import pallas as pl
from jax.experimental.pallas import tpu as pltpu
from jax.sharding import PartitionSpec as P


NSEL = 4
PANEL = 128
PAIR = 2 * PANEL
PLANES = 4
COLS = 8
F32 = jnp.float32


CORE = [(r, r ^ 1) for r in range(16)]
CHIPS = [[r for r in range(16) if r % 2 == core] for core in range(2)]
XPAIR = [(r, r ^ 2) for r in range(16)]
RING = [(r, ((r // 4 + (1 if r % 2 == 0 else 3)) % 4) * 4 + r % 4) for r in range(16)]

VM = pl.BlockSpec()
SM = pl.BlockSpec(memory_space=pltpu.SMEM)
HBM = pl.BlockSpec(memory_space=pltpu.HBM)


def stay(value):
    return pltpu.with_memory_space_constraint(value, pltpu.HBM)


def ordered(first, mine, other):
    low = jnp.where(first, mine, other)
    high = jnp.where(first, other, mine)
    return jnp.concatenate([low, high], axis=0)


def rotate_body(at_ref, *refs):
    for i in range(PLANES):
        refs[PLANES + i][...] = refs[i][...]


def rotate(at, gradient, tile=96):
    rows, width = gradient.shape
    quarter = width // PLANES
    spec = lambda i: pl.BlockSpec((tile, quarter), lambda r, at_ref: (r, at_ref[i]))
    return pl.pallas_call(
        rotate_body,
        grid_spec=pltpu.PrefetchScalarGridSpec(
            num_scalar_prefetch=1,
            grid=(rows // tile,),
            in_specs=[spec(i) for i in range(PLANES)],
            out_specs=[pl.BlockSpec((tile, quarter), lambda r, at_ref: (r, 0))] * PLANES,
        ),
        out_shape=[jax.ShapeDtypeStruct((rows, quarter), F32)] * PLANES,
        compiler_params=pltpu.CompilerParams(vmem_limit_bytes=16 << 20),
        cost_estimate=pl.CostEstimate(flops=1, bytes_accessed=rows * width * 8, transcendentals=0),
        name="rotate",
    )(at, *[stay(gradient)] * PLANES)


def pick_body(at_ref, pieces_ref, mine_ref, give_ref):
    core = at_ref[NSEL]
    for i in range(2):
        mine_ref[i] = pieces_ref[at_ref[2 * core + i] // 2]
        give_ref[i] = pieces_ref[at_ref[2 - 2 * core + i] // 2]


def pick(at, pieces):
    two = jax.ShapeDtypeStruct((2, *pieces.shape[1:]), F32)
    return pl.pallas_call(
        pick_body,
        out_shape=[two, two],
        in_specs=[SM, VM],
        out_specs=[VM] * 2,
        compiler_params=pltpu.CompilerParams(vmem_limit_bytes=8 << 20),
        cost_estimate=pl.CostEstimate(flops=1, bytes_accessed=pieces.size, transcendentals=0),
        name="pick",
    )(at, pieces)


def settle_body(at_ref, mine_ref, got_ref, *outs):
    core = at_ref[NSEL]
    for i, out in enumerate(outs):
        here = at_ref[2 * core + i] % 2 == core

        @pl.when(here)
        def _():
            out[...] = mine_ref[i]

        @pl.when(jnp.logical_not(here))
        def _():
            out[...] = got_ref[i]


def settle(at, mine, got):
    one = jax.ShapeDtypeStruct(mine.shape[1:], F32)
    return pl.pallas_call(
        settle_body,
        out_shape=[one, one],
        in_specs=[SM, VM, VM],
        out_specs=[VM] * 2,
        compiler_params=pltpu.CompilerParams(vmem_limit_bytes=8 << 20),
        cost_estimate=pl.CostEstimate(flops=1, bytes_accessed=mine.size * 8, transcendentals=0),
        name="settle",
    )(at, mine, got)


def place_body(at_ref, *refs):
    v_ref, sems = refs[-2:]
    quarter = refs[0].shape[0]
    moves = []
    for side in range(2):
        for step in range(PLANES):
            rows = pl.ds(pl.multiple_of(at_ref[side * PLANES + step] * quarter, 128), quarter)
            lanes = pl.ds(side * PAIR, PAIR)
            moves.append(pltpu.make_async_copy(refs[side * PLANES + step], v_ref.at[rows, lanes], sems.at[side, step]))
    for move in moves:
        move.start()
    for move in moves:
        move.wait()


def place(at, own, oth):
    quarter = own[0].shape[0]
    return pl.pallas_call(
        place_body,
        out_shape=pltpu.VMEM((PLANES * quarter, 2 * PAIR), F32),
        in_specs=[SM] + [VM] * (2 * PLANES),
        out_specs=VM,
        scratch_shapes=[pltpu.SemaphoreType.DMA((2, PLANES))],
        compiler_params=pltpu.CompilerParams(vmem_limit_bytes=8 << 20),
        cost_estimate=pl.CostEstimate(flops=1, bytes_accessed=quarter * PAIR * 64, transcendentals=0),
        name="place",
    )(at, *own, *oth)


def dot(a, b):
    return jnp.dot(a, b, precision=lax.Precision.HIGH, preferred_element_type=F32)


def across(dy, dx):
    return [(c, ((c // 2 + dy) % 4) * 2 + (c % 2 ^ dx)) for c in range(COLS)]


def shards(gradient, basis, panel_index, input_eigen, output_eigen, input_pick, output_pick):
    rows, _ = gradient.shape
    me = lax.axis_index("rows")
    z, x, core = me // 4, (me // 2) % 2, me % 2
    even = core == 0
    way = jnp.where(even, 1, -1)

    damped = (input_eigen[input_pick] * output_eigen[output_pick] + 0.05).reshape(-1)
    damped = jnp.where(even, damped, jnp.roll(damped, PAIR))

    pieces = lax.all_to_all(basis.reshape(8, -1, PANEL), "rows", 0, 0, axis_index_groups=CHIPS)
    at = jnp.arange(PLANES, dtype=jnp.int32) * way.astype(jnp.int32)
    at = jnp.concatenate([(z - at + 4) % 4, (z + at + 4) % 4])
    pieces, *g = lax.optimization_barrier((pieces, *rotate(at, gradient)))
    chosen = jnp.append(panel_index, core).astype(jnp.int32)
    mine, give = pick(chosen, pieces)
    half_a, half_b = settle(chosen, mine, lax.ppermute(give, "rows", CORE))

    def other_x(half):
        return ordered(x == 0, half, lax.ppermute(half, "rows", XPAIR))

    own, halves = [[other_x(half_a)], []], [half_b]
    for step in range(PLANES - 1):
        halves.append(lax.ppermute(halves[step], "rows", RING))
    own[1] = [other_x(half) for half in halves]

    v_own, v_oth, total, waiting = [], [], None, None

    def product(step, own, oth, total):
        mine, other = jnp.concatenate(own, axis=1), jnp.concatenate(oth, axis=1)
        v_own.append(mine)
        v_oth.append(other)
        mine, other = dot(g[step], mine), dot(g[-step % PLANES], other)
        return (mine, other) if total is None else (total[0] + mine, total[1] + other)

    for step in range(PLANES):
        oth = [None, None]
        for c in range(2):
            held = own[c][step]
            if c == 0 and waiting is not None:
                last_oth = waiting[2]
                if total is not None:
                    held, last_oth[0], *total = lax.optimization_barrier((held, last_oth[0], *total))
                else:
                    held, last_oth[0] = lax.optimization_barrier((held, last_oth[0]))
            if c == 0 and step < PLANES - 1:
                own[c].append(lax.ppermute(held, "rows", RING))
            oth[c] = lax.ppermute(held, "rows", CORE)
        if waiting is not None:
            total = product(*waiting, total)
        waiting = (step, [own[0][step], own[1][step]], oth)
    total = product(*waiting, total)
    p = jnp.concatenate(total, axis=1)
    v = place(at, v_own, v_oth)

    mine = lax.axis_index("cols")
    block = rows // COLS
    turns = [(dy, dx) for dy in (2, 1, 3, 0) for dx in (1, 0)]
    there = [((mine // 2 + dy) % 4) * 2 + (mine % 2 ^ dx) for dy, dx in turns]
    back = [((mine // 2 - dy) % 4) * 2 + (mine % 2 ^ dx) for dy, dx in turns]
    sums = []
    for at_rows, turn in zip(there, turns):
        part = lax.dynamic_slice(p, (at_rows * block, 0), (block, NSEL * PANEL))
        sums.append(part if turn == (0, 0) else lax.ppermute(part, "cols", across(*turn)))
    scaled_block = sum(sums[1:], sums[0]) / damped[None, :]
    scaled = jnp.zeros((rows, NSEL * PANEL), F32)
    for at_rows, turn in zip(back, turns):
        part = scaled_block if turn == (0, 0) else lax.ppermute(scaled_block, "cols", across(*turn))
        scaled = lax.dynamic_update_slice(scaled, part, (at_rows * block, 0))
    return lax.dot_general(
        scaled, v, (((1,), (1,)), ((), ())), precision=lax.Precision.HIGH, preferred_element_type=F32
    )


def solution(mesh):
    in_specs = (P("rows", "cols"), P("rows", "cols", None), P(), P(), P(), P(), P())
    out_specs = P("rows", "cols")

    return jax.shard_map(shards, mesh=mesh, in_specs=in_specs, out_specs=out_specs, check_vma=False)
```

```python
import jax
import jax.numpy as jnp
from jax import lax
from jax.experimental import pallas as pl
from jax.experimental.pallas import tpu as pltpu
from jax.sharding import PartitionSpec as P


NSEL = 4
PANEL = 128
PAIR = 2 * PANEL
PLANES = 4
COLS = 8
F32 = jnp.float32


CORE = [(r, r ^ 1) for r in range(16)]
XPAIR = [(r, r ^ 2) for r in range(16)]
RING = [(r, ((r // 4 + (1 if r % 2 == 0 else 3)) % 4) * 4 + r % 4) for r in range(16)]

VM = pl.BlockSpec()
SM = pl.BlockSpec(memory_space=pltpu.SMEM)
HBM = pl.BlockSpec(memory_space=pltpu.HBM)


def stay(value):
    return pltpu.with_memory_space_constraint(value, pltpu.HBM)


def ordered(first, mine, other):
    low = jnp.where(first, mine, other)
    high = jnp.where(first, other, mine)
    return jnp.concatenate([low, high], axis=0)


def rotate_body(at_ref, *refs):
    for i in range(PLANES):
        refs[PLANES + i][...] = refs[i][...]


def rotate(at, gradient, tile=96):
    rows, width = gradient.shape
    quarter = width // PLANES
    spec = lambda i: pl.BlockSpec((tile, quarter), lambda r, at_ref: (r, at_ref[i]))
    return pl.pallas_call(
        rotate_body,
        grid_spec=pltpu.PrefetchScalarGridSpec(
            num_scalar_prefetch=1,
            grid=(rows // tile,),
            in_specs=[spec(i) for i in range(PLANES)],
            out_specs=[pl.BlockSpec((tile, quarter), lambda r, at_ref: (r, 0))] * PLANES,
        ),
        out_shape=[jax.ShapeDtypeStruct((rows, quarter), F32)] * PLANES,
        compiler_params=pltpu.CompilerParams(vmem_limit_bytes=16 << 20),
        cost_estimate=pl.CostEstimate(flops=1, bytes_accessed=rows * width * 8, transcendentals=0),
        name="rotate",
    )(at, *[stay(gradient)] * PLANES)


def pick_body(at_ref, pieces_ref, a_ref, b_ref, give_ref):
    core = at_ref[NSEL]
    a_ref[...] = pieces_ref[at_ref[2 * core]]
    b_ref[...] = pieces_ref[at_ref[2 * core + 1]]
    give_ref[0] = pieces_ref[at_ref[2 - 2 * core]]
    give_ref[1] = pieces_ref[at_ref[3 - 2 * core]]


def pick(at, pieces):
    one = jax.ShapeDtypeStruct(pieces.shape[1:], F32)
    two = jax.ShapeDtypeStruct((2, *pieces.shape[1:]), F32)
    return pl.pallas_call(
        pick_body,
        out_shape=[one, one, two],
        in_specs=[SM, VM],
        out_specs=[VM] * 3,
        compiler_params=pltpu.CompilerParams(vmem_limit_bytes=8 << 20),
        cost_estimate=pl.CostEstimate(flops=1, bytes_accessed=pieces.size, transcendentals=0),
        name="pick",
    )(at, pieces)


def place_body(at_ref, *refs):
    v_ref, sems = refs[-2:]
    quarter = refs[0].shape[0]
    moves = []
    for side in range(2):
        for step in range(PLANES):
            rows = pl.ds(pl.multiple_of(at_ref[side * PLANES + step] * quarter, 128), quarter)
            lanes = pl.ds(side * PAIR, PAIR)
            moves.append(pltpu.make_async_copy(refs[side * PLANES + step], v_ref.at[rows, lanes], sems.at[side, step]))
    for move in moves:
        move.start()
    for move in moves:
        move.wait()


def place(at, own, oth):
    quarter = own[0].shape[0]
    return pl.pallas_call(
        place_body,
        out_shape=pltpu.VMEM((PLANES * quarter, 2 * PAIR), F32),
        in_specs=[SM] + [VM] * (2 * PLANES),
        out_specs=VM,
        scratch_shapes=[pltpu.SemaphoreType.DMA((2, PLANES))],
        compiler_params=pltpu.CompilerParams(vmem_limit_bytes=8 << 20),
        cost_estimate=pl.CostEstimate(flops=1, bytes_accessed=quarter * PAIR * 64, transcendentals=0),
        name="place",
    )(at, *own, *oth)


def dot(a, b):
    return jnp.dot(a, b, precision=lax.Precision.HIGH, preferred_element_type=F32)


def across(dy, dx):
    return [(c, ((c // 2 + dy) % 4) * 2 + (c % 2 ^ dx)) for c in range(COLS)]


TURNS = ((2, 1), (2, 0), (1, 1), (3, 1), (1, 0), (3, 0), (0, 1), (0, 0))


def shards(gradient, basis, panel_index, input_eigen, output_eigen, input_pick, output_pick):
    rows, _ = gradient.shape
    me = lax.axis_index("rows")
    z, x, core = me // 4, (me // 2) % 2, me % 2
    even = core == 0
    way = jnp.where(even, 1, -1)

    damped = (input_eigen[input_pick] * output_eigen[output_pick] + 0.05).reshape(-1)
    damped = jnp.where(even, damped, jnp.roll(damped, PAIR))

    pieces = lax.all_to_all(basis.reshape(16, -1, PANEL), "rows", 0, 0)
    at = jnp.arange(PLANES, dtype=jnp.int32) * way.astype(jnp.int32)
    at = jnp.concatenate([(z - at + 4) % 4, (z + at + 4) % 4])
    pieces, damped, *g = lax.optimization_barrier((pieces, damped, *rotate(at, gradient)))
    mine_a, mine_b, give = pick(jnp.append(panel_index, core).astype(jnp.int32), pieces)
    got = lax.ppermute(give, "rows", CORE)
    halves = [ordered(even, mine_a, got[0]), ordered(even, mine_b, got[1])]
    own = [[], []]
    for c, half in enumerate(halves):
        own[c].append(ordered(x == 0, half, lax.ppermute(half, "rows", XPAIR)))

    v_own, v_oth, total, waiting = [], [], None, None

    def product(step, own, oth, total):
        mine, other = jnp.concatenate(own, axis=1), jnp.concatenate(oth, axis=1)
        v_own.append(mine)
        v_oth.append(other)
        mine, other = dot(g[step], mine), dot(g[-step % PLANES], other)
        return (mine, other) if total is None else (total[0] + mine, total[1] + other)

    for step in range(PLANES):
        oth = [None, None]
        for c in range(2):
            held = own[c][step]
            if c == 0 and waiting is not None:
                last_oth = waiting[2]
                if total is not None:
                    held, last_oth[0], *total = lax.optimization_barrier((held, last_oth[0], *total))
                else:
                    held, last_oth[0] = lax.optimization_barrier((held, last_oth[0]))
            if step < PLANES - 1:
                own[c].append(lax.ppermute(held, "rows", RING))
            oth[c] = lax.ppermute(held, "rows", CORE)
        if waiting is not None:
            total = product(*waiting, total)
        waiting = (step, [own[0][step], own[1][step]], oth)
    total = product(*waiting, total)
    p = jnp.concatenate(total, axis=1)
    v = place(at, v_own, v_oth)

    mine = lax.axis_index("cols")
    block = rows // COLS
    there = [((mine // 2 + dy) % 4) * 2 + (mine % 2 ^ dx) for dy, dx in TURNS]
    back = [((mine // 2 - dy) % 4) * 2 + (mine % 2 ^ dx) for dy, dx in TURNS]
    sums = []
    for at_rows, turn in zip(there, TURNS):
        part = lax.dynamic_slice(p, (at_rows * block, 0), (block, NSEL * PANEL))
        sums.append(part if turn == (0, 0) else lax.ppermute(part, "cols", across(*turn)))
    v, *sums = lax.optimization_barrier((v, *sums))
    scaled_block = sum(sums[1:], sums[0]) / damped[None, :]
    scaled = jnp.zeros((rows, NSEL * PANEL), F32)
    for at_rows, turn in zip(back, TURNS):
        part = scaled_block if turn == (0, 0) else lax.ppermute(scaled_block, "cols", across(*turn))
        scaled = lax.dynamic_update_slice(scaled, part, (at_rows * block, 0))
    return lax.dot_general(
        scaled, v, (((1,), (1,)), ((), ())), precision=lax.Precision.HIGH, preferred_element_type=F32
    )


def solution(mesh):
    in_specs = (P("rows", "cols"), P("rows", "cols", None), P(), P(), P(), P(), P())
    out_specs = P("rows", "cols")

    return jax.shard_map(shards, mesh=mesh, in_specs=in_specs, out_specs=out_specs, check_vma=False)
```

```python
import jax
import jax.numpy as jnp
from jax import lax
from jax.experimental import pallas as pl
from jax.experimental.pallas import tpu as pltpu
from jax.sharding import PartitionSpec as P


NSEL = 4
PANEL = 128
PAIR = 2 * PANEL
PLANES = 4
COLS = 8
F32 = jnp.float32


CORE = [(r, r ^ 1) for r in range(16)]
XPAIR = [(r, r ^ 2) for r in range(16)]
RING = [(r, ((r // 4 + (1 if r % 2 == 0 else 3)) % 4) * 4 + r % 4) for r in range(16)]

VM = pl.BlockSpec()
SM = pl.BlockSpec(memory_space=pltpu.SMEM)
HBM = pl.BlockSpec(memory_space=pltpu.HBM)


def stay(value):
    return pltpu.with_memory_space_constraint(value, pltpu.HBM)


def ordered(first, mine, other):
    low = jnp.where(first, mine, other)
    high = jnp.where(first, other, mine)
    return jnp.concatenate([low, high], axis=0)


def rotate_body(at_ref, *refs):
    count = len(refs) // 2
    for i in range(count):
        refs[count + i][...] = refs[i][...]


def rotate(at, gradient, steps, tile=96):
    rows, width = gradient.shape
    quarter = width // PLANES
    spec = lambda i: pl.BlockSpec((tile, quarter), lambda r, at_ref: (r, at_ref[i]))
    return pl.pallas_call(
        rotate_body,
        grid_spec=pltpu.PrefetchScalarGridSpec(
            num_scalar_prefetch=1,
            grid=(rows // tile,),
            in_specs=[spec(i) for i in steps],
            out_specs=[pl.BlockSpec((tile, quarter), lambda r, at_ref: (r, 0))] * len(steps),
        ),
        out_shape=[jax.ShapeDtypeStruct((rows, quarter), F32)] * len(steps),
        compiler_params=pltpu.CompilerParams(vmem_limit_bytes=16 << 20),
        cost_estimate=pl.CostEstimate(flops=1, bytes_accessed=rows * quarter * 8 * len(steps), transcendentals=0),
        name="rotate",
    )(at, *[stay(gradient)] * len(steps))


def pick_body(at_ref, *refs):
    pieces, (mine_ref, give_ref) = refs[:-2], refs[-2:]
    core, z, x = at_ref[NSEL], at_ref[NSEL + 1], at_ref[NSEL + 2]
    for i in range(2):
        for out, slot in ((mine_ref, 2 * core + i), (give_ref, 2 - 2 * core + i)):
            panel = at_ref[slot]
            came = ((z + PLANES - panel // 4) % PLANES) * 2 + (x + panel // 2) % 2
            for j, piece in enumerate(pieces):

                @pl.when(came == j)
                def _():
                    out[i] = piece[...]


def pick(at, pieces):
    two = jax.ShapeDtypeStruct((2, *pieces[0].shape), F32)
    return pl.pallas_call(
        pick_body,
        out_shape=[two, two],
        in_specs=[SM] + [VM] * len(pieces),
        out_specs=[VM] * 2,
        compiler_params=pltpu.CompilerParams(vmem_limit_bytes=8 << 20),
        cost_estimate=pl.CostEstimate(flops=1, bytes_accessed=pieces[0].size * 32, transcendentals=0),
        name="pick",
    )(at, *pieces)


def settle_body(at_ref, mine_ref, got_ref, *outs):
    core = at_ref[NSEL]
    for i, out in enumerate(outs):
        here = at_ref[2 * core + i] % 2 == core

        @pl.when(here)
        def _():
            out[...] = mine_ref[i]

        @pl.when(jnp.logical_not(here))
        def _():
            out[...] = got_ref[i]


def settle(at, mine, got):
    one = jax.ShapeDtypeStruct(mine.shape[1:], F32)
    return pl.pallas_call(
        settle_body,
        out_shape=[one, one],
        in_specs=[SM, VM, VM],
        out_specs=[VM] * 2,
        compiler_params=pltpu.CompilerParams(vmem_limit_bytes=8 << 20),
        cost_estimate=pl.CostEstimate(flops=1, bytes_accessed=mine.size * 8, transcendentals=0),
        name="settle",
    )(at, mine, got)


def place_body(at_ref, *refs):
    v_ref, sems = refs[-2:]
    quarter = refs[0].shape[0]
    moves = []
    for side in range(2):
        for step in range(PLANES):
            rows = pl.ds(pl.multiple_of(at_ref[side * PLANES + step] * quarter, 128), quarter)
            lanes = pl.ds(side * PAIR, PAIR)
            moves.append(pltpu.make_async_copy(refs[side * PLANES + step], v_ref.at[rows, lanes], sems.at[side, step]))
    for move in moves:
        move.start()
    for move in moves:
        move.wait()


def place(at, own, oth):
    quarter = own[0].shape[0]
    return pl.pallas_call(
        place_body,
        out_shape=pltpu.VMEM((PLANES * quarter, 2 * PAIR), F32),
        in_specs=[SM] + [HBM] * (2 * PLANES),
        out_specs=VM,
        scratch_shapes=[pltpu.SemaphoreType.DMA((2, PLANES))],
        compiler_params=pltpu.CompilerParams(vmem_limit_bytes=8 << 20),
        cost_estimate=pl.CostEstimate(flops=1, bytes_accessed=quarter * PAIR * 64, transcendentals=0),
        name="place",
    )(at, *[stay(v) for v in (*own, *oth)])


def dot(a, b):
    return jnp.dot(a, b, precision=lax.Precision.HIGH, preferred_element_type=F32)


def away(dz, dx):
    return [(r, ((r // 4 + dz) % 4) * 4 + ((r // 2 % 2) ^ dx) * 2 + r % 2) for r in range(16)]


SPREAD = ((2, 1), (2, 0), (1, 1), (3, 1), (0, 1), (1, 0), (3, 0))


def across(dy, dx):
    return [(c, ((c // 2 + dy) % 4) * 2 + (c % 2 ^ dx)) for c in range(COLS)]


TURNS = ((2, 1), (2, 0), (1, 1), (3, 1), (1, 0), (3, 0), (0, 1), (0, 0))


def shards(gradient, basis, panel_index, input_eigen, output_eigen, input_pick, output_pick):
    rows, _ = gradient.shape
    me = lax.axis_index("rows")
    z, x, core = me // 4, (me // 2) % 2, me % 2
    even = core == 0
    way = jnp.where(even, 1, -1)

    damped = (input_eigen[input_pick] * output_eigen[output_pick] + 0.05).reshape(-1)
    damped = jnp.where(even, damped, jnp.roll(damped, PAIR))

    at = jnp.arange(PLANES, dtype=jnp.int32) * way.astype(jnp.int32)
    at = jnp.concatenate([(z - at + 4) % 4, (z + at + 4) % 4])

    deep = basis.shape[1] // (2 * PLANES)
    eighth = lambda dz, dx: lax.dynamic_slice(
        basis[0], ((((z + dz) % 4) * 2 + (x ^ dx)) * deep, 0), (deep, PANEL))
    arrived = {(0, 0): eighth(0, 0)}
    for dz, dx in SPREAD:
        arrived[dz, dx] = lax.ppermute(eighth(dz, dx), "rows", away(dz, dx))
    pieces = [arrived[dz, dx] for dz in range(PLANES) for dx in range(2)]
    g = rotate(at, gradient, (0, 1))
    *pieces, g0, g1 = lax.optimization_barrier((*pieces, *g))
    chosen = jnp.concatenate([panel_index, jnp.stack([core, z, x]).astype(jnp.int32)])
    mine, give = pick(chosen, pieces)
    halves = settle(chosen, mine, lax.ppermute(give, "rows", CORE))
    own = [[], []]
    for c, half in enumerate(halves):
        own[c].append(ordered(x == 0, half, lax.ppermute(half, "rows", XPAIR)))

    g = rotate(at, gradient, (2, 3))
    own[0][0], g2, g3 = lax.optimization_barrier((own[0][0], *g))
    g = [g0, g1, g2, g3]

    v_own, v_oth, total, waiting = [], [], None, None

    def product(step, own, oth, total):
        mine, other = jnp.concatenate(own, axis=1), jnp.concatenate(oth, axis=1)
        v_own.append(mine)
        v_oth.append(other)
        mine, other = dot(g[step], mine), dot(g[-step % PLANES], other)
        return (mine, other) if total is None else (total[0] + mine, total[1] + other)

    for step in range(PLANES):
        oth = [None, None]
        for c in range(2):
            held = own[c][step]
            if c == 0 and waiting is not None:
                last_oth = waiting[2]
                if total is not None:
                    held, last_oth[0], *total = lax.optimization_barrier((held, last_oth[0], *total))
                else:
                    held, last_oth[0] = lax.optimization_barrier((held, last_oth[0]))
            if step < PLANES - 1:
                own[c].append(lax.ppermute(held, "rows", RING))
                if (c, step) == (0, 0):
                    own[0][1], damped = lax.optimization_barrier((own[0][1], damped))
            oth[c] = lax.ppermute(held, "rows", CORE)
        if waiting is not None:
            total = product(*waiting, total)
        waiting = (step, [own[0][step], own[1][step]], oth)
    total = product(*waiting, total)
    p = jnp.concatenate(total, axis=1)
    v = place(at, v_own, v_oth)

    mine = lax.axis_index("cols")
    block = rows // COLS
    there = [((mine // 2 + dy) % 4) * 2 + (mine % 2 ^ dx) for dy, dx in TURNS]
    back = [((mine // 2 - dy) % 4) * 2 + (mine % 2 ^ dx) for dy, dx in TURNS]
    sums = []
    for at_rows, turn in zip(there, TURNS):
        part = lax.dynamic_slice(p, (at_rows * block, 0), (block, NSEL * PANEL))
        sums.append(part if turn == (0, 0) else lax.ppermute(part, "cols", across(*turn)))
    scaled_block = sum(sums[1:], sums[0]) / damped[None, :]
    scaled = jnp.zeros((rows, NSEL * PANEL), F32)
    for at_rows, turn in zip(back, TURNS):
        part = scaled_block if turn == (0, 0) else lax.ppermute(scaled_block, "cols", across(*turn))
        scaled = lax.dynamic_update_slice(scaled, part, (at_rows * block, 0))
    return lax.dot_general(
        scaled, v, (((1,), (1,)), ((), ())), precision=lax.Precision.HIGH, preferred_element_type=F32
    )


def solution(mesh):
    in_specs = (P("rows", "cols"), P("rows", "cols", None), P(), P(), P(), P(), P())
    out_specs = P("rows", "cols")

    return jax.shard_map(shards, mesh=mesh, in_specs=in_specs, out_specs=out_specs, check_vma=False)
```

```python
import jax
import jax.numpy as jnp
from jax import lax
from jax.experimental import pallas as pl
from jax.experimental.pallas import tpu as pltpu
from jax.sharding import PartitionSpec as P


NSEL = 4
PANEL = 128
PAIR = 2 * PANEL
PLANES = 4
COLS = 8
F32 = jnp.float32


CORE = [(r, r ^ 1) for r in range(16)]
XPAIR = [(r, r ^ 2) for r in range(16)]
RING = [(r, ((r // 4 + (1 if r % 2 == 0 else 3)) % 4) * 4 + r % 4) for r in range(16)]

VM = pl.BlockSpec()
SM = pl.BlockSpec(memory_space=pltpu.SMEM)
HBM = pl.BlockSpec(memory_space=pltpu.HBM)


def stay(value):
    return pltpu.with_memory_space_constraint(value, pltpu.HBM)


def ordered(first, mine, other):
    low = jnp.where(first, mine, other)
    high = jnp.where(first, other, mine)
    return jnp.concatenate([low, high], axis=0)


def rotate_body(at_ref, *refs):
    count = len(refs) // 2
    for i in range(count):
        refs[count + i][...] = refs[i][...]


def rotate(at, gradient, steps, tile=96):
    rows, width = gradient.shape
    quarter = width // PLANES
    spec = lambda i: pl.BlockSpec((tile, quarter), lambda r, at_ref: (r, at_ref[i]))
    return pl.pallas_call(
        rotate_body,
        grid_spec=pltpu.PrefetchScalarGridSpec(
            num_scalar_prefetch=1,
            grid=(rows // tile,),
            in_specs=[spec(i) for i in steps],
            out_specs=[pl.BlockSpec((tile, quarter), lambda r, at_ref: (r, 0))] * len(steps),
        ),
        out_shape=[jax.ShapeDtypeStruct((rows, quarter), F32)] * len(steps),
        compiler_params=pltpu.CompilerParams(vmem_limit_bytes=16 << 20),
        cost_estimate=pl.CostEstimate(flops=1, bytes_accessed=rows * quarter * 8 * len(steps), transcendentals=0),
        name="rotate",
    )(at, *[stay(gradient)] * len(steps))


def pick_body(at_ref, *refs):
    pieces, (mine_ref, give_ref) = refs[:-2], refs[-2:]
    core, z, x = at_ref[NSEL], at_ref[NSEL + 1], at_ref[NSEL + 2]
    for i in range(2):
        for out, slot in ((mine_ref, 2 * core + i), (give_ref, 2 - 2 * core + i)):
            panel = at_ref[slot]
            came = ((z + PLANES - panel // 4) % PLANES) * 2 + (x + panel // 2) % 2
            for j, piece in enumerate(pieces):

                @pl.when(came == j)
                def _():
                    out[i] = piece[...]


def pick(at, pieces):
    two = jax.ShapeDtypeStruct((2, *pieces[0].shape), F32)
    return pl.pallas_call(
        pick_body,
        out_shape=[two, two],
        in_specs=[SM] + [VM] * len(pieces),
        out_specs=[VM] * 2,
        compiler_params=pltpu.CompilerParams(vmem_limit_bytes=8 << 20),
        cost_estimate=pl.CostEstimate(flops=1, bytes_accessed=pieces[0].size * 32, transcendentals=0),
        name="pick",
    )(at, *pieces)


def settle_body(at_ref, mine_ref, got_ref, *outs):
    core = at_ref[NSEL]
    for i, out in enumerate(outs):
        here = at_ref[2 * core + i] % 2 == core

        @pl.when(here)
        def _():
            out[...] = mine_ref[i]

        @pl.when(jnp.logical_not(here))
        def _():
            out[...] = got_ref[i]


def settle(at, mine, got):
    one = jax.ShapeDtypeStruct(mine.shape[1:], F32)
    return pl.pallas_call(
        settle_body,
        out_shape=[one, one],
        in_specs=[SM, VM, VM],
        out_specs=[VM] * 2,
        compiler_params=pltpu.CompilerParams(vmem_limit_bytes=8 << 20),
        cost_estimate=pl.CostEstimate(flops=1, bytes_accessed=mine.size * 8, transcendentals=0),
        name="settle",
    )(at, mine, got)


def place_body(at_ref, *refs):
    v_ref, sems = refs[-2:]
    quarter = refs[0].shape[0]
    moves = []
    for side in range(2):
        for step in range(PLANES):
            rows = pl.ds(pl.multiple_of(at_ref[side * PLANES + step] * quarter, 128), quarter)
            lanes = pl.ds(side * PAIR, PAIR)
            moves.append(pltpu.make_async_copy(refs[side * PLANES + step], v_ref.at[rows, lanes], sems.at[side, step]))
    for move in moves:
        move.start()
    for move in moves:
        move.wait()


def place(at, own, oth):
    quarter = own[0].shape[0]
    return pl.pallas_call(
        place_body,
        out_shape=pltpu.VMEM((PLANES * quarter, 2 * PAIR), F32),
        in_specs=[SM] + [HBM] * (2 * PLANES),
        out_specs=VM,
        scratch_shapes=[pltpu.SemaphoreType.DMA((2, PLANES))],
        compiler_params=pltpu.CompilerParams(vmem_limit_bytes=8 << 20),
        cost_estimate=pl.CostEstimate(flops=1, bytes_accessed=quarter * PAIR * 64, transcendentals=0),
        name="place",
    )(at, *[stay(v) for v in (*own, *oth)])


def dot(a, b):
    return jnp.dot(a, b, precision=lax.Precision.HIGH, preferred_element_type=F32)


def away(dz, dx):
    return [(r, ((r // 4 + dz) % 4) * 4 + ((r // 2 % 2) ^ dx) * 2 + r % 2) for r in range(16)]


SPREAD = ((2, 1), (2, 0), (1, 1), (3, 1), (0, 1), (1, 0), (3, 0))


def across(dy, dx):
    return [(c, ((c // 2 + dy) % 4) * 2 + (c % 2 ^ dx)) for c in range(COLS)]


TURNS = ((2, 1), (2, 0), (1, 1), (3, 1), (1, 0), (3, 0), (0, 1), (0, 0))


def shards(gradient, basis, panel_index, input_eigen, output_eigen, input_pick, output_pick):
    rows, _ = gradient.shape
    me = lax.axis_index("rows")
    z, x, core = me // 4, (me // 2) % 2, me % 2
    even = core == 0
    way = jnp.where(even, 1, -1)

    damped = (input_eigen[input_pick] * output_eigen[output_pick] + 0.05).reshape(-1)
    damped = jnp.where(even, damped, jnp.roll(damped, PAIR))

    at = jnp.arange(PLANES, dtype=jnp.int32) * way.astype(jnp.int32)
    at = jnp.concatenate([(z - at + 4) % 4, (z + at + 4) % 4])

    deep = basis.shape[1] // (2 * PLANES)
    eighth = lambda dz, dx: lax.dynamic_slice(
        basis[0], ((((z + dz) % 4) * 2 + (x ^ dx)) * deep, 0), (deep, PANEL))
    arrived = {(0, 0): eighth(0, 0)}
    for dz, dx in SPREAD:
        arrived[dz, dx] = lax.ppermute(eighth(dz, dx), "rows", away(dz, dx))
    pieces = [arrived[dz, dx] for dz in range(PLANES) for dx in range(2)]
    g = rotate(at, gradient, (0, 1, 3))
    *pieces, g0, g1, g3 = lax.optimization_barrier((*pieces, *g))
    chosen = jnp.concatenate([panel_index, jnp.stack([core, z, x]).astype(jnp.int32)])
    mine, give = pick(chosen, pieces)
    halves = settle(chosen, mine, lax.ppermute(give, "rows", CORE))
    own = [[], []]
    for c, half in enumerate(halves):
        own[c].append(ordered(x == 0, half, lax.ppermute(half, "rows", XPAIR)))

    g = rotate(at, gradient, (2,))
    own[0][0], g2 = lax.optimization_barrier((own[0][0], *g))
    g = [g0, g1, g2, g3]

    v_own, v_oth, total, waiting = [], [], None, None

    def product(step, own, oth, total):
        mine, other = jnp.concatenate(own, axis=1), jnp.concatenate(oth, axis=1)
        mine, = lax.optimization_barrier((mine,))
        other, = lax.optimization_barrier((other,))
        v_own.append(mine)
        v_oth.append(other)
        mine, other = dot(g[step], mine), dot(g[-step % PLANES], other)
        return (mine, other) if total is None else (total[0] + mine, total[1] + other)

    for step in range(PLANES):
        oth = [None, None]
        for c in range(2):
            held = own[c][step]
            if c == 0 and waiting is not None:
                last_oth = waiting[2]
                if total is not None:
                    held, last_oth[0], *total = lax.optimization_barrier((held, last_oth[0], *total))
                else:
                    held, last_oth[0] = lax.optimization_barrier((held, last_oth[0]))
            if step < PLANES - 1:
                own[c].append(lax.ppermute(held, "rows", RING))
            oth[c] = lax.ppermute(held, "rows", CORE)
        if waiting is not None:
            total = product(*waiting, total)
        waiting = (step, [own[0][step], own[1][step]], oth)
    total = product(*waiting, total)
    p = jnp.concatenate(total, axis=1)
    v = place(at, v_own, v_oth)

    mine = lax.axis_index("cols")
    block = rows // COLS
    there = [((mine // 2 + dy) % 4) * 2 + (mine % 2 ^ dx) for dy, dx in TURNS]
    back = [((mine // 2 - dy) % 4) * 2 + (mine % 2 ^ dx) for dy, dx in TURNS]
    sums = []
    for at_rows, turn in zip(there, TURNS):
        part = lax.dynamic_slice(p, (at_rows * block, 0), (block, NSEL * PANEL))
        sums.append(part if turn == (0, 0) else lax.ppermute(part, "cols", across(*turn)))
    scaled_block = sum(sums[1:], sums[0]) / damped[None, :]
    scaled = jnp.zeros((rows, NSEL * PANEL), F32)
    for at_rows, turn in zip(back, TURNS):
        part = scaled_block if turn == (0, 0) else lax.ppermute(scaled_block, "cols", across(*turn))
        scaled = lax.dynamic_update_slice(scaled, part, (at_rows * block, 0))
    return lax.dot_general(
        scaled, v, (((1,), (1,)), ((), ())), precision=lax.Precision.HIGH, preferred_element_type=F32
    )


def solution(mesh):
    in_specs = (P("rows", "cols"), P("rows", "cols", None), P(), P(), P(), P(), P())
    out_specs = P("rows", "cols")

    return jax.shard_map(shards, mesh=mesh, in_specs=in_specs, out_specs=out_specs, check_vma=False)
```

```python
import jax
import jax.numpy as jnp
from jax import lax
from jax.experimental import pallas as pl
from jax.experimental.pallas import tpu as pltpu
from jax.sharding import PartitionSpec as P


NSEL = 4
PANEL = 128
PAIR = 2 * PANEL
PLANES = 4
COLS = 8
F32 = jnp.float32


CORE = [(r, r ^ 1) for r in range(16)]
XPAIR = [(r, r ^ 2) for r in range(16)]
RING = [(r, ((r // 4 + (1 if r % 2 == 0 else 3)) % 4) * 4 + r % 4) for r in range(16)]

VM = pl.BlockSpec()
SM = pl.BlockSpec(memory_space=pltpu.SMEM)
HBM = pl.BlockSpec(memory_space=pltpu.HBM)


def stay(value):
    return pltpu.with_memory_space_constraint(value, pltpu.HBM)


def rotate_body(at_ref, *refs):
    count = len(refs) // 2
    for i in range(count):
        refs[count + i][...] = refs[i][...]


def rotate(at, gradient, steps, tile=96):
    rows, width = gradient.shape
    quarter = width // PLANES
    spec = lambda i: pl.BlockSpec((tile, quarter), lambda r, at_ref: (r, at_ref[i]))
    return pl.pallas_call(
        rotate_body,
        grid_spec=pltpu.PrefetchScalarGridSpec(
            num_scalar_prefetch=1,
            grid=(rows // tile,),
            in_specs=[spec(i) for i in steps],
            out_specs=[pl.BlockSpec((tile, quarter), lambda r, at_ref: (r, 0))] * len(steps),
        ),
        out_shape=[jax.ShapeDtypeStruct((rows, quarter), F32)] * len(steps),
        compiler_params=pltpu.CompilerParams(vmem_limit_bytes=16 << 20),
        cost_estimate=pl.CostEstimate(flops=1, bytes_accessed=rows * quarter * 8 * len(steps), transcendentals=0),
        name="rotate",
    )(at, *[stay(gradient)] * len(steps))


def pick_body(at_ref, *refs):
    pieces, (mine_ref, give_ref) = refs[:-2], refs[-2:]
    core, z, x = at_ref[NSEL], at_ref[NSEL + 1], at_ref[NSEL + 2]
    for i in range(2):
        for out, slot in ((mine_ref, 2 * core + i), (give_ref, 2 - 2 * core + i)):
            panel = at_ref[slot]
            came = ((z + PLANES - panel // 4) % PLANES) * 2 + (x + panel // 2) % 2
            for j, piece in enumerate(pieces):

                @pl.when(came == j)
                def _():
                    out[i] = piece[...]


def pick(at, pieces):
    two = jax.ShapeDtypeStruct((2, *pieces[0].shape), F32)
    return pl.pallas_call(
        pick_body,
        out_shape=[two, two],
        in_specs=[SM] + [VM] * len(pieces),
        out_specs=[VM] * 2,
        compiler_params=pltpu.CompilerParams(vmem_limit_bytes=8 << 20),
        cost_estimate=pl.CostEstimate(flops=1, bytes_accessed=pieces[0].size * 32, transcendentals=0),
        name="pick",
    )(at, *pieces)


def settle_body(at_ref, mine_ref, got_ref, *outs):
    core = at_ref[NSEL]
    for i, out in enumerate(outs):
        here = at_ref[2 * core + i] % 2 == core

        @pl.when(here)
        def _():
            out[...] = mine_ref[i]

        @pl.when(jnp.logical_not(here))
        def _():
            out[...] = got_ref[i]


def settle(at, mine, got):
    one = jax.ShapeDtypeStruct(mine.shape[1:], F32)
    return pl.pallas_call(
        settle_body,
        out_shape=[one, one],
        in_specs=[SM, VM, VM],
        out_specs=[VM] * 2,
        compiler_params=pltpu.CompilerParams(vmem_limit_bytes=8 << 20),
        cost_estimate=pl.CostEstimate(flops=1, bytes_accessed=mine.size * 8, transcendentals=0),
        name="settle",
    )(at, mine, got)


def join_body(at_ref, mine_ref, other_ref, out_ref):
    deep, x = mine_ref.shape[0], at_ref[NSEL + 2]
    out_ref[pl.ds(pl.multiple_of(x * deep, 64), deep)] = mine_ref[...]
    out_ref[pl.ds(pl.multiple_of((1 - x) * deep, 64), deep)] = other_ref[...]


def join(at, mine, other):
    deep, lanes = mine.shape
    return pl.pallas_call(
        join_body,
        out_shape=jax.ShapeDtypeStruct((2 * deep, lanes), F32),
        in_specs=[SM, VM, VM],
        out_specs=VM,
        compiler_params=pltpu.CompilerParams(vmem_limit_bytes=8 << 20),
        cost_estimate=pl.CostEstimate(flops=1, bytes_accessed=mine.size * 16, transcendentals=0),
        name="join",
    )(at, mine, other)


def place_body(at_ref, *refs):
    v_ref, sems = refs[-2:]
    quarter = refs[0].shape[0]
    moves = []
    for side in range(2):
        for step in range(PLANES):
            rows = pl.ds(pl.multiple_of(at_ref[side * PLANES + step] * quarter, 128), quarter)
            lanes = pl.ds(side * PAIR, PAIR)
            moves.append(pltpu.make_async_copy(refs[side * PLANES + step], v_ref.at[rows, lanes], sems.at[side, step]))
    for move in moves:
        move.start()
    for move in moves:
        move.wait()


def place(at, own, oth):
    quarter = own[0].shape[0]
    return pl.pallas_call(
        place_body,
        out_shape=pltpu.VMEM((PLANES * quarter, 2 * PAIR), F32),
        in_specs=[SM] + [HBM] * (2 * PLANES),
        out_specs=VM,
        scratch_shapes=[pltpu.SemaphoreType.DMA((2, PLANES))],
        compiler_params=pltpu.CompilerParams(vmem_limit_bytes=8 << 20),
        cost_estimate=pl.CostEstimate(flops=1, bytes_accessed=quarter * PAIR * 64, transcendentals=0),
        name="place",
    )(at, *[stay(v) for v in (*own, *oth)])


def dot(a, b):
    return jnp.dot(a, b, precision=lax.Precision.HIGH, preferred_element_type=F32)


def away(dz, dx):
    return [(r, ((r // 4 + dz) % 4) * 4 + ((r // 2 % 2) ^ dx) * 2 + r % 2) for r in range(16)]


SPREAD = ((2, 1), (2, 0), (1, 1), (3, 1), (0, 1), (1, 0), (3, 0))


def across(dy, dx):
    return [(c, ((c // 2 + dy) % 4) * 2 + (c % 2 ^ dx)) for c in range(COLS)]


TURNS = ((2, 1), (2, 0), (1, 1), (3, 1), (1, 0), (3, 0), (0, 1), (0, 0))


def shards(gradient, basis, panel_index, input_eigen, output_eigen, input_pick, output_pick):
    rows, _ = gradient.shape
    me = lax.axis_index("rows")
    z, x, core = me // 4, (me // 2) % 2, me % 2
    even = core == 0
    way = jnp.where(even, 1, -1)

    damped = (input_eigen[input_pick] * output_eigen[output_pick] + 0.05).reshape(-1)
    damped = jnp.where(even, damped, jnp.roll(damped, PAIR))

    at = jnp.arange(PLANES, dtype=jnp.int32) * way.astype(jnp.int32)
    at = jnp.concatenate([(z - at + 4) % 4, (z + at + 4) % 4])

    deep = basis.shape[1] // (2 * PLANES)
    eighth = lambda dz, dx: lax.dynamic_slice(
        basis[0], ((((z + dz) % 4) * 2 + (x ^ dx)) * deep, 0), (deep, PANEL))
    arrived = {(0, 0): eighth(0, 0)}
    for dz, dx in SPREAD:
        arrived[dz, dx] = lax.ppermute(eighth(dz, dx), "rows", away(dz, dx))
    pieces = [arrived[dz, dx] for dz in range(PLANES) for dx in range(2)]
    g = rotate(at, gradient, (0, 1, 3))
    *pieces, g0, g1, g3 = lax.optimization_barrier((*pieces, *g))
    chosen = jnp.concatenate([panel_index, jnp.stack([core, z, x]).astype(jnp.int32)])
    mine, give = pick(chosen, pieces)
    halves = settle(chosen, mine, lax.ppermute(give, "rows", CORE))
    own = [[], []]
    for c, half in enumerate(halves):
        own[c].append(join(chosen, half, lax.ppermute(half, "rows", XPAIR)))

    g = rotate(at, gradient, (2,))
    own[0][0], g2 = lax.optimization_barrier((own[0][0], *g))
    g = [g0, g1, g2, g3]

    v_own, v_oth, total, waiting = [], [], None, None

    def product(step, own, oth, total):
        mine, other = jnp.concatenate(own, axis=1), jnp.concatenate(oth, axis=1)
        mine, = lax.optimization_barrier((mine,))
        other, = lax.optimization_barrier((other,))
        v_own.append(mine)
        v_oth.append(other)
        mine, other = dot(g[step], mine), dot(g[-step % PLANES], other)
        return (mine, other) if total is None else (total[0] + mine, total[1] + other)

    for step in range(PLANES):
        oth = [None, None]
        for c in range(2):
            held = own[c][step]
            if c == 0 and waiting is not None:
                last_oth = waiting[2]
                if total is not None:
                    held, last_oth[0], *total = lax.optimization_barrier((held, last_oth[0], *total))
                else:
                    held, last_oth[0] = lax.optimization_barrier((held, last_oth[0]))
            if step < PLANES - 1:
                own[c].append(lax.ppermute(held, "rows", RING))
            oth[c] = lax.ppermute(held, "rows", CORE)
        if waiting is not None:
            total = product(*waiting, total)
        waiting = (step, [own[0][step], own[1][step]], oth)
    total = product(*waiting, total)
    p = jnp.concatenate(total, axis=1)
    v = place(at, v_own, v_oth)

    mine = lax.axis_index("cols")
    block = rows // COLS
    there = [((mine // 2 + dy) % 4) * 2 + (mine % 2 ^ dx) for dy, dx in TURNS]
    back = [((mine // 2 - dy) % 4) * 2 + (mine % 2 ^ dx) for dy, dx in TURNS]
    sums = []
    for at_rows, turn in zip(there, TURNS):
        part = lax.dynamic_slice(p, (at_rows * block, 0), (block, NSEL * PANEL))
        sums.append(part if turn == (0, 0) else lax.ppermute(part, "cols", across(*turn)))
    scaled_block = sum(sums[1:], sums[0]) / damped[None, :]
    scaled = jnp.zeros((rows, NSEL * PANEL), F32)
    for at_rows, turn in zip(back, TURNS):
        part = scaled_block if turn == (0, 0) else lax.ppermute(scaled_block, "cols", across(*turn))
        scaled = lax.dynamic_update_slice(scaled, part, (at_rows * block, 0))
    return lax.dot_general(
        scaled, v, (((1,), (1,)), ((), ())), precision=lax.Precision.HIGH, preferred_element_type=F32
    )


def solution(mesh):
    in_specs = (P("rows", "cols"), P("rows", "cols", None), P(), P(), P(), P(), P())
    out_specs = P("rows", "cols")

    return jax.shard_map(shards, mesh=mesh, in_specs=in_specs, out_specs=out_specs, check_vma=False)
```
